32 devices in a mesh: stream: 16 (over z, y, core), span: 2 (over x).
Axes of the slice: x: 2, y: 2, z: 4, core: 2. Of those that a mesh axis runs over, the one named last changes fastest.
Arguments:
- rhs: float32 [64, 2, 320], P('stream', 'span'), may hold values from -1.5 to 1.5
- lower_block: float32 [64, 2, 320, 320], P('stream', 'span'), may hold values from -1.2 to 0.2
- upper_block: bfloat16 [64, 2, 320, 320], P('stream', 'span'), may hold values from -0.099609375 to 0.099609375
- span_block: bfloat16 [64, 2, 2, 320, 320], P('stream', 'span'), may hold values from -0.099609375 to 0.099609375
Outputs:
- preconditioned: float32 [64, 2, 320], P('stream', 'span')
The draws below stay inside these ranges and needn't reach their ends.
All inputs are finite; a program needn't handle non-finite values.
Results may differ from the reference program's by a relative error of at most 0.0003.
Values sent between devices are 32-bit elements; how exact they have to be, the bound alone decides.
A program may use at most 128 MiB of HBM per device.

```python
import jax
import jax.numpy as jnp
from jax import lax

B = 320
SECTION_TOTAL = 64
NLINE = 2


def draw_lower_block(key, part):
    keys = jax.random.split(key, 7)
    share = 0.5
    rate_low = 0.3
    rate_high = 2.0
    quick_rows = (jax.random.uniform(keys[0], (B,)) < share).astype(jnp.float32)
    rate = jnp.exp(jax.random.uniform(keys[1], (B,), jnp.float32, jnp.log(rate_low), jnp.log(rate_high)))
    spread = jnp.exp(jax.random.uniform(keys[2], (SECTION_TOTAL, NLINE, B), jnp.float32, -0.7, 0.7))
    slow_keep = jnp.exp(-rate * spread / SECTION_TOTAL)
    quick_keep = jax.random.uniform(keys[3], (SECTION_TOTAL, NLINE, B), jnp.float32, 0.2, 0.5)
    keep = quick_rows * quick_keep + (1.0 - quick_rows) * slow_keep
    chosen_equations = jax.random.permutation(keys[4], SECTION_TOTAL)[:min(3, SECTION_TOTAL)]
    message_bundles = jnp.any(jnp.arange(SECTION_TOTAL)[:, None] == chosen_equations[None, :], axis=1)
    division_locations = jax.random.uniform(keys[5], (SECTION_TOTAL,), jnp.float32, 0.5, 0.8)
    multiplier_array = jnp.where(message_bundles, division_locations, 1.0)
    keep = keep * multiplier_array[:, None, None]
    row_scaling = quick_rows * (0.3 / B ** 0.5) + (1.0 - quick_rows) * (0.5 / (B * SECTION_TOTAL) ** 0.5)
    noise = jnp.clip(jax.random.normal(keys[6], (SECTION_TOTAL, NLINE, B, B), jnp.float32), -4.0, 4.0)
    noise = jnp.clip(noise * row_scaling[:, None], -0.1, 0.1)
    block = noise + keep[..., None] * jnp.eye(B, dtype=jnp.float32)
    return (-block).astype(jnp.float32)


def block_levels(key, shape, shards, least, top_value):
    level = 1.0
    for dim, shards_of in shards:
        draws = jax.random.uniform(jax.random.fold_in(jax.random.fold_in(key, 6), dim), (shards_of,), jnp.float32, least / len(shards), top_value / len(shards))
        level = level * jnp.repeat(jnp.exp(draws), shape[dim] // shards_of).reshape((-1,) + (1,) * (len(shape) - 1 - dim))
    return level


def gaussian(rng, shape, scale, bound, shards=(), kind=jnp.bfloat16):
    array = jax.random.normal(rng, shape, jnp.float32) * scale
    if len(shards) > 0:
        array = block_levels(rng, shape, shards, -0.22, 0.18) * array
    return jnp.clip(array, min=-bound, max=bound).astype(kind)


def setup_inputs(seed: int = 0) -> dict:
    streams_of = jax.random.split(jax.random.key(seed), 5)
    return {
        "rhs": gaussian(streams_of[0], (SECTION_TOTAL, NLINE, B), (2.0 / SECTION_TOTAL ** 0.5), 1.5, ((0, 16), (1, 2)), jnp.float32),
        "lower_block": draw_lower_block(jax.random.fold_in(streams_of[4], 71), 0),
        "upper_block": gaussian(streams_of[2], (SECTION_TOTAL, NLINE, B, B), 0.017, 0.099609375, ((0, 16), (1, 2))),
        "span_block": gaussian(streams_of[3], (SECTION_TOTAL, NLINE, 2, B, B), 0.017, 0.099609375, ((0, 16), (1, 2))),
    }


def apply_block(blocks, vector):
    return jnp.einsum('...bc,...c->...b', blocks.astype(jnp.float32), vector, precision=lax.Precision.HIGHEST)


def sweep_chain(offsets, lower_block, start):
    def advance(state, inputs):
        offset, block = inputs
        result = offset - apply_block(block, state)
        return result, result

    _, results = lax.scan(advance, start, (offsets, lower_block))
    return results


def reference(rhs, lower_block, upper_block, span_block):
    zero_state = jnp.zeros((rhs.shape[1], rhs.shape[2]), jnp.float32)
    first = sweep_chain(rhs, lower_block, zero_state)
    downstream = jnp.roll(first, -1, axis=0)
    below = jnp.roll(first, 1, axis=1)
    above = jnp.roll(first, -1, axis=1)
    offsets = rhs - apply_block(upper_block, downstream)
    offsets = offsets - apply_block(span_block[:, :, 0], below) - apply_block(span_block[:, :, 1], above)
    return sweep_chain(offsets, lower_block, first[-1])
```

```python
import functools

import jax
import jax.numpy as jnp
from jax import lax
from jax.experimental import pallas as pl
from jax.experimental.pallas import tpu as pltpu
from jax.sharding import PartitionSpec as P

F32 = jnp.float32
BF16 = jnp.bfloat16
MESH = pl.DeviceIdType.MESH
GROUP = 4
NT = (((1,), (1,)), ((), ()))
NN = (((1,), (0,)), ((), ()))


def rows_of(x):
    high = x.astype(BF16).astype(F32)
    row = lax.broadcasted_iota(jnp.int32, (16, x.shape[1]), 0)
    both = jnp.where(row == 0, high, jnp.where(row == 1, x - high, 0.0))
    return both.astype(BF16)


def product(rows, *parts):
    total = None
    for part in parts:
        term = lax.dot_general(rows, part, NT, preferred_element_type=F32)
        total = term if total is None else total + term
    return jnp.sum(total, axis=0, keepdims=True)


def split(a):
    high = a.astype(BF16)
    return high, (a - high.astype(F32)).astype(BF16)


def compose(later, earlier):
    def dot(a, b):
        return lax.dot_general(a, b, NN, preferred_element_type=F32)

    return (
        dot(later[0], earlier[1]) + dot(later[1], earlier[0]) + dot(later[0], earlier[0])
    )


def kernel(
    streams, spans, rhs_ref, lower_hbm, upper_hbm, span_hbm, out_ref,
    lower, upper, spanb, low_hi, low_lo, maps, maps_hi, maps_lo, group_hi, group_lo,
    offs, vec, start_state, first, down, side, stage,
    load_sem, send_sem, recv_sem,
):
    d = lax.axis_index("stream")
    j = lax.axis_index("span")
    slabs = lower.shape[0]
    size = lower.shape[1]
    half = size // 2
    groups = streams // GROUP
    bit0 = lax.rem(d, 2)
    bit1 = lax.rem(d // 2, 2)
    group = d // GROUP
    pair0 = (d + 1 - 2 * bit0, j)
    pair1 = (d + 2 - 4 * bit1, j)
    ahead = (lax.rem(d + GROUP, streams), j)
    behind = (lax.rem(d + streams - GROUP, streams), j)
    prev = (lax.rem(d + streams - 1, streams), j)
    following = (lax.rem(d + 1, streams), j)
    right = (d, lax.rem(j + 1, spans))
    left = (d, lax.rem(j + spans - 1, spans))

    loads = []
    for i in range(slabs):
        loads.append(pltpu.make_async_copy(lower_hbm.at[i, 0], lower.at[i], load_sem.at[i]))
    loads.append(pltpu.make_async_copy(upper_hbm.at[:, 0], upper, load_sem.at[slabs]))
    loads.append(pltpu.make_async_copy(span_hbm.at[:, 0], spanb, load_sem.at[slabs + 1]))
    for load in loads:
        load.start()

    barrier = pltpu.get_barrier_semaphore()
    partners = [pair0, pair1, ahead, behind, prev, following, right]
    if spans > 2:
        partners.append(left)
    for partner in partners:
        pl.semaphore_signal(barrier, inc=1, device_id=partner, device_id_type=MESH)

    def send(src, dst, number, to, recv_number=None):
        copy = pltpu.make_async_remote_copy(
            src_ref=src, dst_ref=dst, send_sem=send_sem.at[number],
            recv_sem=recv_sem.at[number if recv_number is None else recv_number],
            device_id=to, device_id_type=MESH,
        )
        copy.start()
        return copy

    for i in range(slabs):
        loads[i].wait()
        high, low = split(lower[i])
        low_hi[i] = high
        low_lo[i] = low

    parts = [(low_hi[i], low_lo[i]) for i in range(slabs)]
    while len(parts) > 1:
        following_parts = []
        for k in range(0, len(parts) - 1, 2):
            whole = compose(parts[k + 1], parts[k])
            if len(parts) == 2:
                break
            following_parts.append(split(whole))
        else:
            if len(parts) % 2:
                following_parts.append(parts[-1])
            parts = following_parts
            continue
        break
    if slabs == 1:
        whole = lower[0]
    if slabs % 2:
        whole = -whole
    maps[0, bit0] = whole
    pl.semaphore_wait(barrier, len(partners))
    map_copy = send(maps.at[0, bit0], maps.at[0, bit0], 0, pair0)

    def chain(begin, keep):
        state = begin
        for i in range(slabs):
            if state is None:
                state = offs[i]
            else:
                state = offs[i] - product(rows_of(state), low_hi[i], low_lo[i])
            if keep is not None:
                keep(i, state)
        return state

    def level_product(level, slot, x):
        return product(rows_of(x), maps_hi[level, slot], maps_lo[level, slot])

    def descend(sweep, state):
        wide = jnp.where(bit1 == 1, level_product(1, 0, state) + vec[sweep, 1, 0], state)
        return jnp.where(bit0 == 1, level_product(0, 0, wide) + vec[sweep, 0, 0], wide)

    offs[...] = rhs_ref[...]
    vec[0, 0, bit0] = chain(None, None)
    vec_copies = [send(vec.at[0, 0, bit0], vec.at[0, 0, bit0], 3, pair0)]
    map_copy.wait()
    for slot in range(2):
        high, low = split(maps[0, slot])
        maps_hi[0, slot] = high
        maps_lo[0, slot] = low
    maps[1, bit1] = compose((maps_hi[0, 1], maps_lo[0, 1]), (maps_hi[0, 0], maps_lo[0, 0]))
    mine = pl.ds(bit0 * half, half)
    half_copy = send(maps.at[1, bit1, mine], maps.at[1, bit1, mine], 1, pair1)
    vec_copies[0].wait()
    vec[0, 1, bit1] = vec[0, 0, 1] + level_product(0, 1, vec[0, 0, 0])
    vec_copies.append(send(vec.at[0, 1, bit1], vec.at[0, 1, bit1], 4, pair1))
    half_copy.wait()
    forward_copy = send(
        maps.at[1, 1 - bit1, mine], maps.at[1, 1 - bit1, mine], 2, pair0
    )
    vec_copies[1].wait()
    forward_copy.wait()
    for slot in range(2):
        high, low = split(maps[1, slot])
        maps_hi[1, slot] = high
        maps_lo[1, slot] = low
    shift = vec[0, 1, 1] + level_product(1, 1, vec[0, 1, 0])

    arrival = (group + 1) // groups
    chain_first = pltpu.make_async_remote_copy(
        src_ref=stage.at[0], dst_ref=start_state.at[arrival], send_sem=send_sem.at[7],
        recv_sem=recv_sem.at[7 + arrival], device_id=ahead, device_id_type=MESH,
    )

    def arrived(slot):
        return pltpu.make_async_remote_copy(
            src_ref=stage.at[slot], dst_ref=start_state.at[slot],
            send_sem=send_sem.at[7 + slot], recv_sem=recv_sem.at[7 + slot],
            device_id=ahead, device_id_type=MESH,
        )

    @pl.when(group == 0)
    def _():
        start_state[0] = jnp.zeros((1, size), F32)
        stage[0] = shift
        chain_first.start()

    whole_map = compose((maps_hi[1, 1], maps_lo[1, 1]), (maps_hi[1, 0], maps_lo[1, 0]))
    high, low = split(whole_map)
    group_hi[...] = high
    group_lo[...] = low

    @pl.when(group > 0)
    def _():
        arrived(0).wait_recv()
        stage[0] = shift + product(rows_of(start_state[0]), group_hi[...], group_lo[...])
        chain_first.start()

    def keep_first(i, state):
        first[i] = state

    chain(descend(0, start_state[0]), keep_first)
    side_copies = [send(first, side.at[0], 9, right)]
    if spans > 2:
        side_copies.append(send(first, side.at[1], 10, left))
    down_copy = send(first.at[0], down, 11, prev)
    loads[slabs].wait()
    loads[slabs + 1].wait()
    for copy in side_copies:
        copy.wait()
    down_copy.wait()
    for i in range(slabs):
        downstream = first[i + 1] if i + 1 < slabs else down[...]
        below = rows_of(side[0, i])
        above = below if spans <= 2 else rows_of(side[1, i])
        offs[i] = (
            rhs_ref[i] - product(rows_of(downstream), upper[i])
            - product(below, spanb[i, 0]) - product(above, spanb[i, 1])
        )

    vec[1, 0, bit0] = chain(None, None)
    copy = send(vec.at[1, 0, bit0], vec.at[1, 0, bit0], 5, pair0)
    copy.wait()
    vec[1, 1, bit1] = vec[1, 0, 1] + level_product(0, 1, vec[1, 0, 0])
    copy = send(vec.at[1, 1, bit1], vec.at[1, 1, bit1], 6, pair1)
    copy.wait()
    shift = vec[1, 1, 1] + level_product(1, 1, vec[1, 1, 0])
    arrived(1).wait_recv()

    @pl.when(group < groups - 1)
    def _():
        stage[1] = shift + product(rows_of(start_state[1]), group_hi[...], group_lo[...])
        arrived(1).start()

    def keep_out(i, state):
        out_ref[i] = state

    chain(descend(1, start_state[1]), keep_out)
    chain_first.wait_send()

    @pl.when(group < groups - 1)
    def _():
        arrived(1).wait_send()


def solution(mesh):
    streams, spans = mesh.shape["stream"], mesh.shape["span"]

    def shards(rhs, lower_block, upper_block, span_block):
        slabs, _, size = rhs.shape
        return pl.pallas_call(
            functools.partial(kernel, streams, spans),
            out_shape=jax.ShapeDtypeStruct((slabs, 1, size), F32),
            in_specs=[
                pl.BlockSpec(memory_space=pltpu.VMEM),
                pl.BlockSpec(memory_space=pl.ANY),
                pl.BlockSpec(memory_space=pl.ANY),
                pl.BlockSpec(memory_space=pl.ANY),
            ],
            out_specs=pl.BlockSpec(memory_space=pltpu.VMEM),
            scratch_shapes=[
                pltpu.VMEM((slabs, size, size), F32),
                pltpu.VMEM((slabs, size, size), BF16),
                pltpu.VMEM((slabs, 2, size, size), BF16),
                pltpu.VMEM((slabs, size, size), BF16),
                pltpu.VMEM((slabs, size, size), BF16),
                pltpu.VMEM((2, 2, size, size), F32),
                pltpu.VMEM((2, 2, size, size), BF16),
                pltpu.VMEM((2, 2, size, size), BF16),
                pltpu.VMEM((size, size), BF16),
                pltpu.VMEM((size, size), BF16),
                pltpu.VMEM((slabs, 1, size), F32),
                pltpu.VMEM((2, 2, 2, 1, size), F32),
                pltpu.VMEM((2, 1, size), F32),
                pltpu.VMEM((slabs, 1, size), F32),
                pltpu.VMEM((1, size), F32),
                pltpu.VMEM((2, slabs, 1, size), F32),
                pltpu.VMEM((2, 1, size), F32),
                pltpu.SemaphoreType.DMA((slabs + 2,)),
                pltpu.SemaphoreType.DMA((12,)),
                pltpu.SemaphoreType.DMA((12,)),
            ],
            compiler_params=pltpu.CompilerParams(
                collective_id=0, has_side_effects=True, vmem_limit_bytes=40 * 1024 * 1024
            ),
        )(rhs, lower_block, upper_block, span_block)

    return jax.shard_map(
        shards,
        mesh=mesh,
        in_specs=(
            P("stream", "span", None),
            P("stream", "span", None, None),
            P("stream", "span", None, None),
            P("stream", "span", None, None, None),
        ),
        out_specs=P("stream", "span", None),
        check_vma=False,
    )
```

```python
import functools

import jax
import jax.numpy as jnp
from jax import lax
from jax.experimental import pallas as pl
from jax.experimental.pallas import tpu as pltpu
from jax.sharding import PartitionSpec as P

F32 = jnp.float32
BF16 = jnp.bfloat16
MESH = pl.DeviceIdType.MESH
GROUP = 4
NT = (((1,), (1,)), ((), ()))
NN = (((1,), (0,)), ((), ()))


def columns(a, x):
    return jnp.sum(a * x, axis=1, keepdims=True)


def as_row(column):
    size = column.shape[0]
    pieces = []
    for begin in range(0, size, 128):
        count = min(128, size - begin)
        row = lax.broadcasted_iota(jnp.int32, (count, count), 0)
        lane = lax.broadcasted_iota(jnp.int32, (count, count), 1)
        part = jnp.where(row == lane, column[begin : begin + count], 0.0)
        pieces.append(jnp.sum(part, axis=0, keepdims=True))
    return jnp.concatenate(pieces, axis=1)


def product(a, x):
    return as_row(columns(a, x))


def split(a):
    high = a.astype(BF16)
    return high, (a - high.astype(F32)).astype(BF16)


def compose(later, earlier):
    def dot(a, b):
        return lax.dot_general(a, b, NN, preferred_element_type=F32)

    return (
        dot(later[0], earlier[1]) + dot(later[1], earlier[0]) + dot(later[0], earlier[0])
    )


def kernel(
    streams, spans, rhs_hbm, lower_hbm, upper_hbm, span_hbm, out_ref,
    rhs, lower, upper, spanb, upper_wide, span_wide, maps, group_map,
    offs, vec, start_state, middle, first, down, side, stage,
    load_sem, send_sem, recv_sem,
):
    d = lax.axis_index("stream")
    j = lax.axis_index("span")
    slabs = lower.shape[0]
    size = lower.shape[1]
    half = size // 2
    groups = streams // GROUP
    early = min(2, groups - 1)
    bit0 = lax.rem(d, 2)
    bit1 = lax.rem(d // 2, 2)
    group = d // GROUP
    other = 2 - 4 * bit1
    pair0 = (d + 1 - 2 * bit0, j)
    pair1 = (d + other, j)
    ahead = (lax.rem(d + GROUP, streams), j)
    behind = (lax.rem(d + streams - GROUP, streams), j)
    ahead_pair = (lax.rem(d + GROUP, streams) + other, j)
    behind_pair = (lax.rem(d + streams - GROUP, streams) + other, j)
    prev = (lax.rem(d + streams - 1, streams), j)
    following = (lax.rem(d + 1, streams), j)
    right = (d, lax.rem(j + 1, spans))
    left = (d, lax.rem(j + spans - 1, spans))

    loads = []
    for i in range(slabs):
        loads.append(pltpu.make_async_copy(lower_hbm.at[i, 0], lower.at[i], load_sem.at[i]))
    rhs_load = pltpu.make_async_copy(rhs_hbm, rhs, load_sem.at[slabs + 2])
    upper_load = pltpu.make_async_copy(upper_hbm.at[:, 0], upper, load_sem.at[slabs])
    span_load = pltpu.make_async_copy(span_hbm.at[:, 0], spanb, load_sem.at[slabs + 1])
    loads[0].start()
    rhs_load.start()
    for load in loads[1:]:
        load.start()
    upper_load.start()
    span_load.start()

    barrier = pltpu.get_barrier_semaphore()
    partners = [
        pair0, pair1, ahead, behind, ahead_pair, behind_pair, prev, following, right
    ]
    if spans > 2:
        partners.append(left)
    for partner in partners:
        pl.semaphore_signal(barrier, inc=1, device_id=partner, device_id_type=MESH)

    def remote(src, dst, number, to, recv_number=None):
        return pltpu.make_async_remote_copy(
            src_ref=src, dst_ref=dst, send_sem=send_sem.at[number],
            recv_sem=recv_sem.at[number if recv_number is None else recv_number],
            device_id=to, device_id_type=MESH,
        )

    def send(src, dst, number, to):
        copy = remote(src, dst, number, to)
        copy.start()
        return copy

    parts = []
    for i in range(slabs):
        loads[i].wait()
        part = split(lower[i])
        if i % 2:
            whole = compose(part, pending)
            if slabs > 2:
                parts.append(split(whole))
        else:
            pending = part
    if slabs == 1:
        whole = lower[0]
    elif slabs > 2:
        if slabs % 2:
            parts.append(pending)
        rest = parts[0]
        for k in range(1, len(parts)):
            whole = compose(parts[k], rest)
            if k < len(parts) - 1:
                rest = split(whole)
    if slabs % 2:
        whole = -whole
    maps[0, bit0] = whole
    pl.semaphore_wait(barrier, len(partners))
    map_copy = send(maps.at[0, bit0], maps.at[0, bit0], 0, pair0)

    def chain(begin, keep):
        state = begin
        for i in range(slabs):
            if state is None:
                state = offs[i]
            else:
                state = offs[i] - product(lower[i], state)
            if keep is not None:
                keep(i, state)
        return state

    def descend(sweep, state):
        wide = jnp.where(bit1 == 1, product(maps[1, 0], state) + vec[sweep, 1, 0], state)
        return jnp.where(bit0 == 1, product(maps[0, 0], wide) + vec[sweep, 0, 0], wide)

    rhs_load.wait()
    offs[...] = rhs[...]
    vec[0, 0, bit0] = chain(None, None)
    pair0_copy = send(vec.at[0, 0, bit0], vec.at[0, 0, bit0], 3, pair0)
    map_copy.wait_recv()
    pair_map = compose(split(maps[0, 1]), split(maps[0, 0]))
    maps[1, bit1] = pair_map
    mine = pl.ds(bit0 * half, half)
    half_copy = send(maps.at[1, bit1, mine], maps.at[1, bit1, mine], 1, pair1)
    pair0_copy.wait_recv()
    vec[0, 1, bit1] = vec[0, 0, 1] + product(maps[0, 1], vec[0, 0, 0])
    pair1_copy = send(vec.at[0, 1, bit1], vec.at[0, 1, bit1], 4, pair1)

    upper_load.wait()
    span_load.wait()
    for i in range(slabs):
        upper_wide[i] = upper[i].astype(F32)
        if spans <= 2:
            span_wide[i] = spanb[i, 0].astype(F32) + spanb[i, 1].astype(F32)

    arrival = (group + 1) // groups
    chain_first = remote(stage.at[0], start_state.at[arrival], 7, ahead, 7 + arrival)
    chain_other = remote(stage.at[0], start_state.at[0], 12, ahead_pair, 7)
    middle_copy = remote(stage.at[2], middle, 13, pair1)

    def arrived(slot):
        return remote(stage.at[slot], start_state.at[slot], 7 + slot, ahead)

    pair1_copy.wait_recv()

    @pl.when(group == 0)
    def _():
        start_state[0] = jnp.zeros((1, size), F32)

    @pl.when((group == 0) & (bit1 == 1))
    def _():
        stage[0] = vec[0, 1, 1] + product(maps[1, 1], vec[0, 1, 0])
        chain_first.start()
        chain_other.start()

    if early > 1:
        @pl.when((group == 1) & (bit1 == 0))
        def _():
            arrived(0).wait_recv()
            stage[2] = vec[0, 1, 0] + product(maps[1, 0], start_state[0])
            middle_copy.start()

        @pl.when((group == 1) & (bit1 == 1))
        def _():
            middle_copy.wait_recv()
            stage[0] = vec[0, 1, 1] + product(maps[1, 1], middle[...])
            chain_first.start()
            chain_other.start()
            arrived(0).wait_recv()

    half_copy.wait_recv()
    forward_copy = send(
        maps.at[1, 1 - bit1, mine], maps.at[1, 1 - bit1, mine], 2, pair0
    )
    forward_copy.wait_recv()
    shift = vec[0, 1, 1] + product(maps[1, 1], vec[0, 1, 0])
    group_map[...] = compose(split(maps[1, 1]), split(maps[1, 0]))

    @pl.when(group >= early)
    def _():
        arrived(0).wait_recv()
        stage[0] = shift + product(group_map[...], start_state[0])
        chain_first.start()

    def keep_first(i, state):
        first[i] = state

    chain(descend(0, start_state[0]), keep_first)
    side_copies = [send(first, side.at[0], 9, right)]
    if spans > 2:
        side_copies.append(send(first, side.at[1], 10, left))
    down_copy = send(first.at[0], down, 11, prev)
    for copy in side_copies:
        copy.wait_recv()
    down_copy.wait_recv()
    for i in range(slabs):
        total = upper_wide[i] * (first[i + 1] if i + 1 < slabs else down[...])
        if spans <= 2:
            total = total + span_wide[i] * side[0, i]
        else:
            total = total + spanb[i, 0].astype(F32) * side[0, i]
            total = total + spanb[i, 1].astype(F32) * side[1, i]
        offs[i] = rhs[i] - as_row(jnp.sum(total, axis=1, keepdims=True))

    vec[1, 0, bit0] = chain(None, None)
    second0 = send(vec.at[1, 0, bit0], vec.at[1, 0, bit0], 5, pair0)
    second0.wait_recv()
    vec[1, 1, bit1] = vec[1, 0, 1] + product(maps[0, 1], vec[1, 0, 0])
    second1 = send(vec.at[1, 1, bit1], vec.at[1, 1, bit1], 6, pair1)
    second1.wait_recv()
    shift = vec[1, 1, 1] + product(maps[1, 1], vec[1, 1, 0])
    arrived(1).wait_recv()

    @pl.when(group < groups - 1)
    def _():
        stage[1] = shift + product(group_map[...], start_state[1])
        arrived(1).start()

    def keep_out(i, state):
        out_ref[i] = state

    chain(descend(1, start_state[1]), keep_out)
    for copy in side_copies + [
        map_copy, half_copy, forward_copy, pair0_copy, pair1_copy, down_copy, second0, second1
    ]:
        copy.wait_send()

    @pl.when((group >= early) | (bit1 == 1))
    def _():
        chain_first.wait_send()

    @pl.when((group < early) & (bit1 == 1))
    def _():
        chain_other.wait_send()

    if early > 1:
        @pl.when((group == 1) & (bit1 == 0))
        def _():
            middle_copy.wait_send()

    @pl.when(group < groups - 1)
    def _():
        arrived(1).wait_send()


def solution(mesh):
    streams, spans = mesh.shape["stream"], mesh.shape["span"]

    def shards(rhs, lower_block, upper_block, span_block):
        slabs, _, size = rhs.shape
        return pl.pallas_call(
            functools.partial(kernel, streams, spans),
            out_shape=jax.ShapeDtypeStruct((slabs, 1, size), F32),
            in_specs=[pl.BlockSpec(memory_space=pltpu.HBM)] * 4,
            out_specs=pl.BlockSpec(memory_space=pltpu.VMEM),
            scratch_shapes=[
                pltpu.VMEM((slabs, 1, size), F32),
                pltpu.VMEM((slabs, size, size), F32),
                pltpu.VMEM((slabs, size, size), BF16),
                pltpu.VMEM((slabs, 2, size, size), BF16),
                pltpu.VMEM((slabs, size, size), F32),
                pltpu.VMEM((slabs, size, size), F32),
                pltpu.VMEM((2, 2, size, size), F32),
                pltpu.VMEM((size, size), F32),
                pltpu.VMEM((slabs, 1, size), F32),
                pltpu.VMEM((2, 2, 2, 1, size), F32),
                pltpu.VMEM((2, 1, size), F32),
                pltpu.VMEM((1, size), F32),
                pltpu.VMEM((slabs, 1, size), F32),
                pltpu.VMEM((1, size), F32),
                pltpu.VMEM((2, slabs, 1, size), F32),
                pltpu.VMEM((3, 1, size), F32),
                pltpu.SemaphoreType.DMA((slabs + 3,)),
                pltpu.SemaphoreType.DMA((14,)),
                pltpu.SemaphoreType.DMA((14,)),
            ],
            compiler_params=pltpu.CompilerParams(
                collective_id=0, has_side_effects=True, vmem_limit_bytes=63 * 1024 * 1024
            ),
        )(rhs, lower_block, upper_block, span_block)

    return jax.shard_map(
        shards,
        mesh=mesh,
        in_specs=(
            P("stream", "span", None),
            P("stream", "span", None, None),
            P("stream", "span", None, None),
            P("stream", "span", None, None, None),
        ),
        out_specs=P("stream", "span", None),
        check_vma=False,
    )
```

```python
import functools

import jax
import jax.numpy as jnp
from jax import lax
from jax.experimental import pallas as pl
from jax.experimental.pallas import tpu as pltpu
from jax.sharding import PartitionSpec as P

F32 = jnp.float32
BF16 = jnp.bfloat16
MESH = pl.DeviceIdType.MESH
GROUP = 4
NT = (((1,), (1,)), ((), ()))
NN = (((1,), (0,)), ((), ()))


def columns(a, x):
    return jnp.sum(a * x, axis=1, keepdims=True)


def as_row(column):
    size = column.shape[0]
    pieces = []
    for begin in range(0, size, 128):
        count = min(128, size - begin)
        row = lax.broadcasted_iota(jnp.int32, (count, count), 0)
        lane = lax.broadcasted_iota(jnp.int32, (count, count), 1)
        part = jnp.where(row == lane, column[begin : begin + count], 0.0)
        pieces.append(jnp.sum(part, axis=0, keepdims=True))
    return jnp.concatenate(pieces, axis=1)


def product(a, x):
    return as_row(columns(a, x))


def split(a):
    high = a.astype(BF16)
    return high, (a - high.astype(F32)).astype(BF16)


def compose(later, earlier):
    def dot(a, b):
        return lax.dot_general(a, b, NN, preferred_element_type=F32)

    return (
        dot(later[0], earlier[1]) + dot(later[1], earlier[0]) + dot(later[0], earlier[0])
    )


def kernel(
    streams, spans, rhs_hbm, lower_hbm, upper_hbm, span_hbm, out_ref,
    rhs, lower, upper, spanb, upper_wide, span_wide, maps, group_map,
    offs, vec, start_state, middle, first, down, side, stage,
    load_sem, send_sem, recv_sem,
):
    d = lax.axis_index("stream")
    j = lax.axis_index("span")
    slabs = lower.shape[0]
    size = lower.shape[1]
    half = size // 2
    groups = streams // GROUP
    early = min(2, groups - 1)
    bit0 = lax.rem(d, 2)
    bit1 = lax.rem(d // 2, 2)
    group = d // GROUP
    other = 2 - 4 * bit1
    pair0 = (d + 1 - 2 * bit0, j)
    pair1 = (d + other, j)
    ahead = (lax.rem(d + GROUP, streams), j)
    behind = (lax.rem(d + streams - GROUP, streams), j)
    ahead_pair = (lax.rem(d + GROUP, streams) + other, j)
    behind_pair = (lax.rem(d + streams - GROUP, streams) + other, j)
    across = (d + other + 1 - 2 * bit0, j)
    prev = (lax.rem(d + streams - 1, streams), j)
    following = (lax.rem(d + 1, streams), j)
    right = (d, lax.rem(j + 1, spans))
    left = (d, lax.rem(j + spans - 1, spans))

    loads = []
    for i in range(slabs):
        loads.append(pltpu.make_async_copy(lower_hbm.at[i, 0], lower.at[i], load_sem.at[i]))
    rhs_load = pltpu.make_async_copy(rhs_hbm, rhs, load_sem.at[slabs + 2])
    upper_load = pltpu.make_async_copy(upper_hbm.at[:, 0], upper, load_sem.at[slabs])
    span_load = pltpu.make_async_copy(span_hbm.at[:, 0], spanb, load_sem.at[slabs + 1])
    loads[0].start()
    rhs_load.start()
    for load in loads[1:]:
        load.start()
    upper_load.start()
    span_load.start()

    barrier = pltpu.get_barrier_semaphore()
    partners = [
        pair0, pair1, ahead, behind, ahead_pair, behind_pair, prev, following, right,
        across,
    ]
    if spans > 2:
        partners.append(left)
    for partner in partners:
        pl.semaphore_signal(barrier, inc=1, device_id=partner, device_id_type=MESH)

    def remote(src, dst, number, to, recv_number=None):
        return pltpu.make_async_remote_copy(
            src_ref=src, dst_ref=dst, send_sem=send_sem.at[number],
            recv_sem=recv_sem.at[number if recv_number is None else recv_number],
            device_id=to, device_id_type=MESH,
        )

    def send(src, dst, number, to):
        copy = remote(src, dst, number, to)
        copy.start()
        return copy

    def chain(begin, keep):
        state = begin
        for i in range(slabs):
            if state is None:
                state = offs[i]
            else:
                state = offs[i] - product(lower[i], state)
            if keep is not None:
                keep(i, state)
        return state

    def descend(sweep, state):
        wide = jnp.where(bit1 == 1, product(maps[1, 0], state) + vec[sweep, 1, 0], state)
        return jnp.where(bit0 == 1, product(maps[0, 0], wide) + vec[sweep, 0, 0], wide)

    parts = []
    for i in range(slabs):
        loads[i].wait()
        part = split(lower[i])
        if i % 2:
            whole = compose(part, pending)
            if slabs > 2:
                parts.append(split(whole))
        else:
            pending = part
    rhs_load.wait()
    offs[...] = rhs[...]
    vec[0, 0, bit0] = chain(None, None)
    pl.semaphore_wait(barrier, len(partners))
    pair0_copy = send(vec.at[0, 0, bit0], vec.at[0, 0, bit0], 3, pair0)
    if slabs == 1:
        whole = lower[0]
    elif slabs > 2:
        if slabs % 2:
            parts.append(pending)
        rest = parts[0]
        for k in range(1, len(parts)):
            whole = compose(parts[k], rest)
            if k < len(parts) - 1:
                rest = split(whole)
    if slabs % 2:
        whole = -whole
    maps[0, bit0] = whole
    map_copy = send(maps.at[0, bit0], maps.at[0, bit0], 0, pair0)

    pair1_copy = remote(vec.at[0, 1, bit1], vec.at[0, 1, bit1], 4, pair1)
    across_copy = remote(vec.at[0, 1, bit1], vec.at[0, 1, bit1], 14, across, 4)
    pair0_copy.wait_recv()

    @pl.when(bit0 == 1)
    def _():
        vec[0, 1, bit1] = vec[0, 0, 1] + product(maps[0, 1], vec[0, 0, 0])
        pair1_copy.start()
        across_copy.start()

    map_copy.wait_recv()

    @pl.when(bit0 == 0)
    def _():
        vec[0, 1, bit1] = vec[0, 0, 1] + product(maps[0, 1], vec[0, 0, 0])

    pair_map = compose(split(maps[0, 1]), split(maps[0, 0]))
    maps[1, bit1] = pair_map
    mine = pl.ds(bit0 * half, half)
    half_copy = send(maps.at[1, bit1, mine], maps.at[1, bit1, mine], 1, pair1)

    upper_load.wait()
    span_load.wait()
    for i in range(slabs):
        upper_wide[i] = upper[i].astype(F32)
        if spans <= 2:
            span_wide[i] = spanb[i, 0].astype(F32) + spanb[i, 1].astype(F32)

    arrival = (group + 1) // groups
    chain_first = remote(stage.at[0], start_state.at[arrival], 7, ahead, 7 + arrival)
    chain_other = remote(stage.at[0], start_state.at[0], 12, ahead_pair, 7)
    middle_copy = remote(stage.at[2], middle, 13, pair1)

    def arrived(slot):
        return remote(stage.at[slot], start_state.at[slot], 7 + slot, ahead)

    pair1_copy.wait_recv()

    @pl.when(group == 0)
    def _():
        start_state[0] = jnp.zeros((1, size), F32)

    @pl.when((group == 0) & (bit1 == 1))
    def _():
        stage[0] = vec[0, 1, 1] + product(maps[1, 1], vec[0, 1, 0])
        chain_first.start()
        chain_other.start()

    if early > 1:
        @pl.when((group == 1) & (bit1 == 0))
        def _():
            arrived(0).wait_recv()
            stage[2] = vec[0, 1, 0] + product(maps[1, 0], start_state[0])
            middle_copy.start()

        @pl.when((group == 1) & (bit1 == 1))
        def _():
            middle_copy.wait_recv()
            stage[0] = vec[0, 1, 1] + product(maps[1, 1], middle[...])
            chain_first.start()
            chain_other.start()
            arrived(0).wait_recv()

    half_copy.wait_recv()
    forward_copy = send(
        maps.at[1, 1 - bit1, mine], maps.at[1, 1 - bit1, mine], 2, pair0
    )
    forward_copy.wait_recv()
    shift = vec[0, 1, 1] + product(maps[1, 1], vec[0, 1, 0])
    group_map[...] = compose(split(maps[1, 1]), split(maps[1, 0]))

    @pl.when(group >= early)
    def _():
        arrived(0).wait_recv()
        stage[0] = shift + product(group_map[...], start_state[0])
        chain_first.start()

    def keep_first(i, state):
        first[i] = state

    chain(descend(0, start_state[0]), keep_first)
    side_copies = [send(first, side.at[0], 9, right)]
    if spans > 2:
        side_copies.append(send(first, side.at[1], 10, left))
    down_copy = send(first.at[0], down, 11, prev)
    for copy in side_copies:
        copy.wait_recv()
    down_copy.wait_recv()
    for i in range(slabs):
        total = upper_wide[i] * (first[i + 1] if i + 1 < slabs else down[...])
        if spans <= 2:
            total = total + span_wide[i] * side[0, i]
        else:
            total = total + spanb[i, 0].astype(F32) * side[0, i]
            total = total + spanb[i, 1].astype(F32) * side[1, i]
        offs[i] = rhs[i] - as_row(jnp.sum(total, axis=1, keepdims=True))

    vec[1, 0, bit0] = chain(None, None)
    second0 = send(vec.at[1, 0, bit0], vec.at[1, 0, bit0], 5, pair0)
    second0.wait_recv()
    vec[1, 1, bit1] = vec[1, 0, 1] + product(maps[0, 1], vec[1, 0, 0])
    second1 = send(vec.at[1, 1, bit1], vec.at[1, 1, bit1], 6, pair1)
    second1.wait_recv()
    shift = vec[1, 1, 1] + product(maps[1, 1], vec[1, 1, 0])
    arrived(1).wait_recv()

    @pl.when(group < groups - 1)
    def _():
        stage[1] = shift + product(group_map[...], start_state[1])
        arrived(1).start()

    def keep_out(i, state):
        out_ref[i] = state

    chain(descend(1, start_state[1]), keep_out)
    for copy in side_copies + [
        map_copy, half_copy, forward_copy, pair0_copy, down_copy, second0, second1
    ]:
        copy.wait_send()

    @pl.when(bit0 == 1)
    def _():
        pair1_copy.wait_send()
        across_copy.wait_send()

    @pl.when((group >= early) | (bit1 == 1))
    def _():
        chain_first.wait_send()

    @pl.when((group < early) & (bit1 == 1))
    def _():
        chain_other.wait_send()

    if early > 1:
        @pl.when((group == 1) & (bit1 == 0))
        def _():
            middle_copy.wait_send()

    @pl.when(group < groups - 1)
    def _():
        arrived(1).wait_send()


def solution(mesh):
    streams, spans = mesh.shape["stream"], mesh.shape["span"]

    def shards(rhs, lower_block, upper_block, span_block):
        slabs, _, size = rhs.shape
        return pl.pallas_call(
            functools.partial(kernel, streams, spans),
            out_shape=jax.ShapeDtypeStruct((slabs, 1, size), F32),
            in_specs=[pl.BlockSpec(memory_space=pltpu.HBM)] * 4,
            out_specs=pl.BlockSpec(memory_space=pltpu.VMEM),
            scratch_shapes=[
                pltpu.VMEM((slabs, 1, size), F32),
                pltpu.VMEM((slabs, size, size), F32),
                pltpu.VMEM((slabs, size, size), BF16),
                pltpu.VMEM((slabs, 2, size, size), BF16),
                pltpu.VMEM((slabs, size, size), F32),
                pltpu.VMEM((slabs, size, size), F32),
                pltpu.VMEM((2, 2, size, size), F32),
                pltpu.VMEM((size, size), F32),
                pltpu.VMEM((slabs, 1, size), F32),
                pltpu.VMEM((2, 2, 2, 1, size), F32),
                pltpu.VMEM((2, 1, size), F32),
                pltpu.VMEM((1, size), F32),
                pltpu.VMEM((slabs, 1, size), F32),
                pltpu.VMEM((1, size), F32),
                pltpu.VMEM((2, slabs, 1, size), F32),
                pltpu.VMEM((3, 1, size), F32),
                pltpu.SemaphoreType.DMA((slabs + 3,)),
                pltpu.SemaphoreType.DMA((15,)),
                pltpu.SemaphoreType.DMA((15,)),
            ],
            compiler_params=pltpu.CompilerParams(
                collective_id=0, has_side_effects=True, vmem_limit_bytes=63 * 1024 * 1024
            ),
        )(rhs, lower_block, upper_block, span_block)

    return jax.shard_map(
        shards,
        mesh=mesh,
        in_specs=(
            P("stream", "span", None),
            P("stream", "span", None, None),
            P("stream", "span", None, None),
            P("stream", "span", None, None, None),
        ),
        out_specs=P("stream", "span", None),
        check_vma=False,
    )
```

```python
import functools

import jax
import jax.numpy as jnp
from jax import lax
from jax.experimental import pallas as pl
from jax.experimental.pallas import tpu as pltpu
from jax.sharding import PartitionSpec as P

F32 = jnp.float32
BF16 = jnp.bfloat16
MESH = pl.DeviceIdType.MESH
GROUP = 4
NT = (((1,), (1,)), ((), ()))
NN = (((1,), (0,)), ((), ()))


def columns(a, x):
    return jnp.sum(a * x, axis=1, keepdims=True)


def as_row(column):
    size = column.shape[0]
    pieces = []
    for begin in range(0, size, 128):
        count = min(128, size - begin)
        row = lax.broadcasted_iota(jnp.int32, (count, count), 0)
        lane = lax.broadcasted_iota(jnp.int32, (count, count), 1)
        part = jnp.where(row == lane, column[begin : begin + count], 0.0)
        pieces.append(jnp.sum(part, axis=0, keepdims=True))
    return jnp.concatenate(pieces, axis=1)


def product(a, x):
    return as_row(columns(a, x))


def split(a):
    high = a.astype(BF16)
    return high, (a - high.astype(F32)).astype(BF16)


def compose(later, earlier):
    def dot(a, b):
        return lax.dot_general(a, b, NN, preferred_element_type=F32)

    return (
        dot(later[0], earlier[1]) + dot(later[1], earlier[0]) + dot(later[0], earlier[0])
    )


def kernel(
    streams, spans, rhs_hbm, lower_hbm, upper_hbm, span_hbm, out_ref,
    rhs, lower, upper, spanb, upper_wide, span_wide, maps, group_map,
    offs, vec, start_state, middle, first, down, side, stage,
    load_sem, send_sem, recv_sem,
):
    d = lax.axis_index("stream")
    j = lax.axis_index("span")
    slabs = lower.shape[0]
    size = lower.shape[1]
    half = size // 2
    groups = streams // GROUP
    early = min(2, groups - 1)
    bit0 = lax.rem(d, 2)
    bit1 = lax.rem(d // 2, 2)
    group = d // GROUP
    other = 2 - 4 * bit1
    pair0 = (d + 1 - 2 * bit0, j)
    pair1 = (d + other, j)
    ahead = (lax.rem(d + GROUP, streams), j)
    behind = (lax.rem(d + streams - GROUP, streams), j)
    ahead_pair = (lax.rem(d + GROUP, streams) + other, j)
    behind_pair = (lax.rem(d + streams - GROUP, streams) + other, j)
    across = (d + other + 1 - 2 * bit0, j)
    prev = (lax.rem(d + streams - 1, streams), j)
    following = (lax.rem(d + 1, streams), j)
    right = (d, lax.rem(j + 1, spans))
    left = (d, lax.rem(j + spans - 1, spans))

    loads = []
    for i in range(slabs):
        loads.append(pltpu.make_async_copy(lower_hbm.at[i, 0], lower.at[i], load_sem.at[i]))
    rhs_load = pltpu.make_async_copy(rhs_hbm, rhs, load_sem.at[slabs + 2])
    upper_load = pltpu.make_async_copy(upper_hbm.at[:, 0], upper, load_sem.at[slabs])
    span_load = pltpu.make_async_copy(span_hbm.at[:, 0], spanb, load_sem.at[slabs + 1])
    loads[0].start()
    rhs_load.start()
    for load in loads[1:]:
        load.start()

    barrier = pltpu.get_barrier_semaphore()
    partners = [
        pair0, pair1, ahead, behind, ahead_pair, behind_pair, prev, following, right,
        across,
    ]
    if spans > 2:
        partners.append(left)
    for partner in partners:
        pl.semaphore_signal(barrier, inc=1, device_id=partner, device_id_type=MESH)

    def remote(src, dst, number, to, recv_number=None):
        return pltpu.make_async_remote_copy(
            src_ref=src, dst_ref=dst, send_sem=send_sem.at[number],
            recv_sem=recv_sem.at[number if recv_number is None else recv_number],
            device_id=to, device_id_type=MESH,
        )

    def send(src, dst, number, to):
        copy = remote(src, dst, number, to)
        copy.start()
        return copy

    def chain(begin, keep):
        state = begin
        for i in range(slabs):
            if state is None:
                state = offs[i]
            else:
                state = offs[i] - product(lower[i], state)
            if keep is not None:
                keep(i, state)
        return state

    def descend(sweep, state):
        wide = jnp.where(bit1 == 1, product(maps[1, 0], state) + vec[sweep, 1, 0], state)
        return jnp.where(bit0 == 1, product(maps[0, 0], wide) + vec[sweep, 0, 0], wide)

    parts = []
    for i in range(slabs):
        loads[i].wait()
        part = split(lower[i])
        if i % 2:
            whole = compose(part, pending)
            if slabs > 2:
                parts.append(split(whole))
        else:
            pending = part
    upper_load.start()
    span_load.start()
    rhs_load.wait()
    offs[...] = rhs[...]
    vec[0, 0, bit0] = chain(None, None)
    pl.semaphore_wait(barrier, len(partners))
    pair0_copy = send(vec.at[0, 0, bit0], vec.at[0, 0, bit0], 3, pair0)
    last = None
    if slabs == 1:
        whole = lower[0]
    elif slabs > 2:
        if slabs % 2:
            parts.append(pending)
        rest = parts[0]
        for k in range(1, len(parts) - 1):
            rest = split(compose(parts[k], rest))
        last = parts[-1]
    map_copies = []
    for k in range(2):
        rows = slice(k * half, (k + 1) * half)
        if last is None:
            piece = whole[rows]
        else:
            piece = compose((last[0][rows], last[1][rows]), rest)
        maps[0, bit0, rows] = -piece if slabs % 2 else piece
        map_copies.append(
            send(maps.at[0, bit0, rows], maps.at[0, bit0, rows], 15 * k, pair0)
        )

    pair1_copy = remote(vec.at[0, 1, bit1], vec.at[0, 1, bit1], 4, pair1)
    across_copy = remote(vec.at[0, 1, bit1], vec.at[0, 1, bit1], 14, across, 4)
    pair0_copy.wait_recv()

    @pl.when(bit0 == 1)
    def _():
        vec[0, 1, bit1] = vec[0, 0, 1] + product(maps[0, 1], vec[0, 0, 0])
        pair1_copy.start()
        across_copy.start()

    for copy in map_copies:
        copy.wait_recv()

    @pl.when(bit0 == 0)
    def _():
        vec[0, 1, bit1] = vec[0, 0, 1] + product(maps[0, 1], vec[0, 0, 0])

    pair_map = compose(split(maps[0, 1]), split(maps[0, 0]))
    maps[1, bit1] = pair_map
    mine = pl.ds(bit0 * half, half)
    half_copy = send(maps.at[1, bit1, mine], maps.at[1, bit1, mine], 1, pair1)

    upper_load.wait()
    span_load.wait()
    for i in range(slabs):
        upper_wide[i] = upper[i].astype(F32)
        if spans <= 2:
            span_wide[i] = spanb[i, 0].astype(F32) + spanb[i, 1].astype(F32)

    arrival = (group + 1) // groups
    chain_first = remote(stage.at[0], start_state.at[arrival], 7, ahead, 7 + arrival)
    chain_other = remote(stage.at[0], start_state.at[0], 12, ahead_pair, 7)
    middle_copy = remote(stage.at[2], middle, 13, pair1)

    def arrived(slot):
        return remote(stage.at[slot], start_state.at[slot], 7 + slot, ahead)

    pair1_copy.wait_recv()

    @pl.when(group == 0)
    def _():
        start_state[0] = jnp.zeros((1, size), F32)

    @pl.when((group == 0) & (bit1 == 1))
    def _():
        stage[0] = vec[0, 1, 1] + product(maps[1, 1], vec[0, 1, 0])
        chain_first.start()
        chain_other.start()

    if early > 1:
        @pl.when((group == 1) & (bit1 == 0))
        def _():
            arrived(0).wait_recv()
            stage[2] = vec[0, 1, 0] + product(maps[1, 0], start_state[0])
            middle_copy.start()

        @pl.when((group == 1) & (bit1 == 1))
        def _():
            middle_copy.wait_recv()
            stage[0] = vec[0, 1, 1] + product(maps[1, 1], middle[...])
            chain_first.start()
            chain_other.start()
            arrived(0).wait_recv()

    half_copy.wait_recv()
    forward_copy = send(
        maps.at[1, 1 - bit1, mine], maps.at[1, 1 - bit1, mine], 2, pair0
    )
    forward_copy.wait_recv()
    shift = vec[0, 1, 1] + product(maps[1, 1], vec[0, 1, 0])
    group_map[...] = compose(split(maps[1, 1]), split(maps[1, 0]))

    @pl.when(group >= early)
    def _():
        arrived(0).wait_recv()
        stage[0] = shift + product(group_map[...], start_state[0])
        chain_first.start()

    def keep_first(i, state):
        first[i] = state

    chain(descend(0, start_state[0]), keep_first)
    side_copies = [send(first, side.at[0], 9, right)]
    if spans > 2:
        side_copies.append(send(first, side.at[1], 10, left))
    down_copy = send(first.at[0], down, 11, prev)
    for copy in side_copies:
        copy.wait_recv()
    down_copy.wait_recv()
    for i in range(slabs):
        total = upper_wide[i] * (first[i + 1] if i + 1 < slabs else down[...])
        if spans <= 2:
            total = total + span_wide[i] * side[0, i]
        else:
            total = total + spanb[i, 0].astype(F32) * side[0, i]
            total = total + spanb[i, 1].astype(F32) * side[1, i]
        offs[i] = rhs[i] - as_row(jnp.sum(total, axis=1, keepdims=True))

    vec[1, 0, bit0] = chain(None, None)
    second0 = send(vec.at[1, 0, bit0], vec.at[1, 0, bit0], 5, pair0)
    second0.wait_recv()
    vec[1, 1, bit1] = vec[1, 0, 1] + product(maps[0, 1], vec[1, 0, 0])
    second1 = send(vec.at[1, 1, bit1], vec.at[1, 1, bit1], 6, pair1)
    second1.wait_recv()
    shift = vec[1, 1, 1] + product(maps[1, 1], vec[1, 1, 0])
    arrived(1).wait_recv()

    @pl.when(group < groups - 1)
    def _():
        stage[1] = shift + product(group_map[...], start_state[1])
        arrived(1).start()

    def keep_out(i, state):
        out_ref[i] = state

    chain(descend(1, start_state[1]), keep_out)
    for copy in side_copies + map_copies + [
        half_copy, forward_copy, pair0_copy, down_copy, second0, second1
    ]:
        copy.wait_send()

    @pl.when(bit0 == 1)
    def _():
        pair1_copy.wait_send()
        across_copy.wait_send()

    @pl.when((group >= early) | (bit1 == 1))
    def _():
        chain_first.wait_send()

    @pl.when((group < early) & (bit1 == 1))
    def _():
        chain_other.wait_send()

    if early > 1:
        @pl.when((group == 1) & (bit1 == 0))
        def _():
            middle_copy.wait_send()

    @pl.when(group < groups - 1)
    def _():
        arrived(1).wait_send()


def solution(mesh):
    streams, spans = mesh.shape["stream"], mesh.shape["span"]

    def shards(rhs, lower_block, upper_block, span_block):
        slabs, _, size = rhs.shape
        return pl.pallas_call(
            functools.partial(kernel, streams, spans),
            out_shape=jax.ShapeDtypeStruct((slabs, 1, size), F32),
            in_specs=[pl.BlockSpec(memory_space=pltpu.HBM)] * 4,
            out_specs=pl.BlockSpec(memory_space=pltpu.VMEM),
            scratch_shapes=[
                pltpu.VMEM((slabs, 1, size), F32),
                pltpu.VMEM((slabs, size, size), F32),
                pltpu.VMEM((slabs, size, size), BF16),
                pltpu.VMEM((slabs, 2, size, size), BF16),
                pltpu.VMEM((slabs, size, size), F32),
                pltpu.VMEM((slabs, size, size), F32),
                pltpu.VMEM((2, 2, size, size), F32),
                pltpu.VMEM((size, size), F32),
                pltpu.VMEM((slabs, 1, size), F32),
                pltpu.VMEM((2, 2, 2, 1, size), F32),
                pltpu.VMEM((2, 1, size), F32),
                pltpu.VMEM((1, size), F32),
                pltpu.VMEM((slabs, 1, size), F32),
                pltpu.VMEM((1, size), F32),
                pltpu.VMEM((2, slabs, 1, size), F32),
                pltpu.VMEM((3, 1, size), F32),
                pltpu.SemaphoreType.DMA((slabs + 3,)),
                pltpu.SemaphoreType.DMA((16,)),
                pltpu.SemaphoreType.DMA((16,)),
            ],
            compiler_params=pltpu.CompilerParams(
                collective_id=0, has_side_effects=True, vmem_limit_bytes=63 * 1024 * 1024
            ),
        )(rhs, lower_block, upper_block, span_block)

    return jax.shard_map(
        shards,
        mesh=mesh,
        in_specs=(
            P("stream", "span", None),
            P("stream", "span", None, None),
            P("stream", "span", None, None),
            P("stream", "span", None, None, None),
        ),
        out_specs=P("stream", "span", None),
        check_vma=False,
    )
```

```python
import functools

import jax
import jax.numpy as jnp
from jax import lax
from jax.experimental import pallas as pl
from jax.experimental.pallas import tpu as pltpu
from jax.sharding import PartitionSpec as P

F32 = jnp.float32
BF16 = jnp.bfloat16
MESH = pl.DeviceIdType.MESH
GROUP = 4
NT = (((1,), (1,)), ((), ()))
NN = (((1,), (0,)), ((), ()))


def columns(a, x):
    return jnp.sum(a * x, axis=1, keepdims=True)


def as_row(column):
    size = column.shape[0]
    pieces = []
    for begin in range(0, size, 128):
        count = min(128, size - begin)
        row = lax.broadcasted_iota(jnp.int32, (count, count), 0)
        lane = lax.broadcasted_iota(jnp.int32, (count, count), 1)
        part = jnp.where(row == lane, column[begin : begin + count], 0.0)
        pieces.append(jnp.sum(part, axis=0, keepdims=True))
    return jnp.concatenate(pieces, axis=1)


def product(a, x):
    return as_row(columns(a, x))


def split(a):
    high = a.astype(BF16)
    return high, (a - high.astype(F32)).astype(BF16)


def compose(later, earlier):
    def dot(a, b):
        return lax.dot_general(a, b, NN, preferred_element_type=F32)

    return (
        dot(later[0], earlier[1]) + dot(later[1], earlier[0]) + dot(later[0], earlier[0])
    )


def kernel(
    streams, spans, rhs_hbm, lower_hbm, upper_hbm, span_hbm, out_ref,
    rhs, lower, upper, spanb, upper_wide, span_wide, maps, group_map,
    offs, vec, start_state, middle, first, down, side, stage,
    load_sem, send_sem, recv_sem,
):
    d = lax.axis_index("stream")
    j = lax.axis_index("span")
    slabs = lower.shape[0]
    size = lower.shape[1]
    half = size // 2
    groups = streams // GROUP
    early = min(2, groups - 1)
    bit0 = lax.rem(d, 2)
    bit1 = lax.rem(d // 2, 2)
    group = d // GROUP
    other = 2 - 4 * bit1
    pair0 = (d + 1 - 2 * bit0, j)
    pair1 = (d + other, j)
    ahead = (lax.rem(d + GROUP, streams), j)
    behind = (lax.rem(d + streams - GROUP, streams), j)
    ahead_pair = (lax.rem(d + GROUP, streams) + other, j)
    behind_pair = (lax.rem(d + streams - GROUP, streams) + other, j)
    across = (d + other + 1 - 2 * bit0, j)
    prev = (lax.rem(d + streams - 1, streams), j)
    following = (lax.rem(d + 1, streams), j)
    right = (d, lax.rem(j + 1, spans))
    left = (d, lax.rem(j + spans - 1, spans))

    loads = []
    for i in range(slabs):
        loads.append(pltpu.make_async_copy(lower_hbm.at[i, 0], lower.at[i], load_sem.at[i]))
    rhs_load = pltpu.make_async_copy(rhs_hbm, rhs, load_sem.at[slabs + 2])
    upper_load = pltpu.make_async_copy(upper_hbm.at[:, 0], upper, load_sem.at[slabs])
    span_load = pltpu.make_async_copy(span_hbm.at[:, 0], spanb, load_sem.at[slabs + 1])
    loads[0].start()
    rhs_load.start()
    for load in loads[1:]:
        load.start()

    barrier = pltpu.get_barrier_semaphore()
    partners = [
        pair0, pair1, ahead, behind, ahead_pair, behind_pair, prev, following, right,
        across,
    ]
    if spans > 2:
        partners.append(left)
    for partner in partners:
        pl.semaphore_signal(barrier, inc=1, device_id=partner, device_id_type=MESH)

    def remote(src, dst, number, to, recv_number=None):
        return pltpu.make_async_remote_copy(
            src_ref=src, dst_ref=dst, send_sem=send_sem.at[number],
            recv_sem=recv_sem.at[number if recv_number is None else recv_number],
            device_id=to, device_id_type=MESH,
        )

    def send(src, dst, number, to):
        copy = remote(src, dst, number, to)
        copy.start()
        return copy

    def chain(begin, keep):
        state = begin
        for i in range(slabs):
            if state is None:
                state = offs[i]
            else:
                state = offs[i] - product(lower[i], state)
            if keep is not None:
                keep(i, state)
        return state

    def descend(sweep, state):
        wide = jnp.where(bit1 == 1, product(maps[1, 0], state) + vec[sweep, 1, 0], state)
        return jnp.where(bit0 == 1, product(maps[0, 0], wide) + vec[sweep, 0, 0], wide)

    parts = []
    for i in range(slabs):
        loads[i].wait()
        part = split(lower[i])
        if i % 2:
            whole = compose(part, pending)
            if slabs > 2:
                parts.append(split(whole))
        else:
            pending = part
    upper_load.start()
    span_load.start()
    rhs_load.wait()
    offs[...] = rhs[...]
    vec[0, 0, bit0] = chain(None, None)
    pl.semaphore_wait(barrier, len(partners))
    pair0_copy = send(vec.at[0, 0, bit0], vec.at[0, 0, bit0], 3, pair0)
    last = None
    if slabs == 1:
        whole = lower[0]
    elif slabs > 2:
        if slabs % 2:
            parts.append(pending)
        rest = parts[0]
        for k in range(1, len(parts) - 1):
            rest = split(compose(parts[k], rest))
        last = parts[-1]
    map_copies = []
    for k in range(2):
        rows = slice(k * half, (k + 1) * half)
        if last is None:
            piece = whole[rows]
        else:
            piece = compose((last[0][rows], last[1][rows]), rest)
        maps[0, bit0, rows] = -piece if slabs % 2 else piece
        map_copies.append(
            send(maps.at[0, bit0, rows], maps.at[0, bit0, rows], 15 * k, pair0)
        )

    pair1_copy = remote(vec.at[0, 1, bit1], vec.at[0, 1, bit1], 4, pair1)
    across_copy = remote(vec.at[0, 1, bit1], vec.at[0, 1, bit1], 14, across, 4)
    pair0_copy.wait_recv()

    @pl.when(bit0 == 1)
    def _():
        vec[0, 1, bit1] = vec[0, 0, 1] + product(maps[0, 1], vec[0, 0, 0])
        pair1_copy.start()
        across_copy.start()

    for copy in map_copies:
        copy.wait_recv()

    @pl.when(bit0 == 0)
    def _():
        vec[0, 1, bit1] = vec[0, 0, 1] + product(maps[0, 1], vec[0, 0, 0])

    earlier = split(maps[0, 0])
    mine = pl.ds(pl.multiple_of(bit0 * half, 8), half)
    rest_rows = pl.ds(pl.multiple_of((1 - bit0) * half, 8), half)
    maps[1, bit1, mine] = compose(split(maps[0, 1, mine]), earlier)
    half_copy = send(maps.at[1, bit1, mine], maps.at[1, bit1, mine], 1, pair1)
    maps[1, bit1, rest_rows] = compose(split(maps[0, 1, rest_rows]), earlier)

    upper_load.wait()
    span_load.wait()
    for i in range(slabs):
        upper_wide[i] = upper[i].astype(F32)
        if spans <= 2:
            span_wide[i] = spanb[i, 0].astype(F32) + spanb[i, 1].astype(F32)

    arrival = (group + 1) // groups
    chain_first = remote(stage.at[0], start_state.at[arrival], 7, ahead, 7 + arrival)
    chain_other = remote(stage.at[0], start_state.at[0], 12, ahead_pair, 7)
    middle_copy = remote(stage.at[2], middle, 13, pair1)

    def arrived(slot):
        return remote(stage.at[slot], start_state.at[slot], 7 + slot, ahead)

    pair1_copy.wait_recv()

    @pl.when(group == 0)
    def _():
        start_state[0] = jnp.zeros((1, size), F32)

    @pl.when((group == 0) & (bit1 == 1))
    def _():
        stage[0] = vec[0, 1, 1] + product(maps[1, 1], vec[0, 1, 0])
        chain_first.start()
        chain_other.start()

    if early > 1:
        @pl.when((group == 1) & (bit1 == 0))
        def _():
            arrived(0).wait_recv()
            stage[2] = vec[0, 1, 0] + product(maps[1, 0], start_state[0])
            middle_copy.start()

        @pl.when((group == 1) & (bit1 == 1))
        def _():
            middle_copy.wait_recv()
            stage[0] = vec[0, 1, 1] + product(maps[1, 1], middle[...])
            chain_first.start()
            chain_other.start()
            arrived(0).wait_recv()

    half_copy.wait_recv()
    forward_copy = send(
        maps.at[1, 1 - bit1, mine], maps.at[1, 1 - bit1, mine], 2, pair0
    )
    forward_copy.wait_recv()
    shift = vec[0, 1, 1] + product(maps[1, 1], vec[0, 1, 0])
    group_map[...] = compose(split(maps[1, 1]), split(maps[1, 0]))

    @pl.when(group >= early)
    def _():
        arrived(0).wait_recv()
        stage[0] = shift + product(group_map[...], start_state[0])
        chain_first.start()

    def keep_first(i, state):
        first[i] = state

    chain(descend(0, start_state[0]), keep_first)
    side_copies = [send(first, side.at[0], 9, right)]
    if spans > 2:
        side_copies.append(send(first, side.at[1], 10, left))
    down_copy = send(first.at[0], down, 11, prev)
    for copy in side_copies:
        copy.wait_recv()
    down_copy.wait_recv()
    for i in range(slabs):
        total = upper_wide[i] * (first[i + 1] if i + 1 < slabs else down[...])
        if spans <= 2:
            total = total + span_wide[i] * side[0, i]
        else:
            total = total + spanb[i, 0].astype(F32) * side[0, i]
            total = total + spanb[i, 1].astype(F32) * side[1, i]
        offs[i] = rhs[i] - as_row(jnp.sum(total, axis=1, keepdims=True))

    vec[1, 0, bit0] = chain(None, None)
    second0 = send(vec.at[1, 0, bit0], vec.at[1, 0, bit0], 5, pair0)
    second0.wait_recv()
    vec[1, 1, bit1] = vec[1, 0, 1] + product(maps[0, 1], vec[1, 0, 0])
    second1 = send(vec.at[1, 1, bit1], vec.at[1, 1, bit1], 6, pair1)
    second1.wait_recv()
    shift = vec[1, 1, 1] + product(maps[1, 1], vec[1, 1, 0])
    arrived(1).wait_recv()

    @pl.when(group < groups - 1)
    def _():
        stage[1] = shift + product(group_map[...], start_state[1])
        arrived(1).start()

    def keep_out(i, state):
        out_ref[i] = state

    chain(descend(1, start_state[1]), keep_out)
    for copy in side_copies + map_copies + [
        half_copy, forward_copy, pair0_copy, down_copy, second0, second1
    ]:
        copy.wait_send()

    @pl.when(bit0 == 1)
    def _():
        pair1_copy.wait_send()
        across_copy.wait_send()

    @pl.when((group >= early) | (bit1 == 1))
    def _():
        chain_first.wait_send()

    @pl.when((group < early) & (bit1 == 1))
    def _():
        chain_other.wait_send()

    if early > 1:
        @pl.when((group == 1) & (bit1 == 0))
        def _():
            middle_copy.wait_send()

    @pl.when(group < groups - 1)
    def _():
        arrived(1).wait_send()


def solution(mesh):
    streams, spans = mesh.shape["stream"], mesh.shape["span"]

    def shards(rhs, lower_block, upper_block, span_block):
        slabs, _, size = rhs.shape
        return pl.pallas_call(
            functools.partial(kernel, streams, spans),
            out_shape=jax.ShapeDtypeStruct((slabs, 1, size), F32),
            in_specs=[pl.BlockSpec(memory_space=pltpu.HBM)] * 4,
            out_specs=pl.BlockSpec(memory_space=pltpu.VMEM),
            scratch_shapes=[
                pltpu.VMEM((slabs, 1, size), F32),
                pltpu.VMEM((slabs, size, size), F32),
                pltpu.VMEM((slabs, size, size), BF16),
                pltpu.VMEM((slabs, 2, size, size), BF16),
                pltpu.VMEM((slabs, size, size), F32),
                pltpu.VMEM((slabs, size, size), F32),
                pltpu.VMEM((2, 2, size, size), F32),
                pltpu.VMEM((size, size), F32),
                pltpu.VMEM((slabs, 1, size), F32),
                pltpu.VMEM((2, 2, 2, 1, size), F32),
                pltpu.VMEM((2, 1, size), F32),
                pltpu.VMEM((1, size), F32),
                pltpu.VMEM((slabs, 1, size), F32),
                pltpu.VMEM((1, size), F32),
                pltpu.VMEM((2, slabs, 1, size), F32),
                pltpu.VMEM((3, 1, size), F32),
                pltpu.SemaphoreType.DMA((slabs + 3,)),
                pltpu.SemaphoreType.DMA((16,)),
                pltpu.SemaphoreType.DMA((16,)),
            ],
            compiler_params=pltpu.CompilerParams(
                collective_id=0, has_side_effects=True, vmem_limit_bytes=63 * 1024 * 1024
            ),
        )(rhs, lower_block, upper_block, span_block)

    return jax.shard_map(
        shards,
        mesh=mesh,
        in_specs=(
            P("stream", "span", None),
            P("stream", "span", None, None),
            P("stream", "span", None, None),
            P("stream", "span", None, None, None),
        ),
        out_specs=P("stream", "span", None),
        check_vma=False,
    )
```
